32 devices in a mesh: rows: 8 (over y, x, core), cols: 4 (over z).
Axes of the slice: x: 2, y: 2, z: 4, core: 2. Of those that a mesh axis runs over, the one named last changes fastest.
Arguments:
- raw_panel: float32 [256, 32768], P('cols', 'rows')
- raw_trail: float32 [1024, 32768], P('cols', 'rows')
- panel_shift: int32 [256], P('cols'), may hold values from 0 to 255, as said below
- trail_shift: int32 [1024], P('cols'), may hold values from 0 to 255, as said below
Outputs:
- r_factor: float32 [256, 256], replicated
- coupling: float32 [256, 1024], P(None, 'cols')
- q_panel: float32 [256, 32768], P('cols', 'rows')
- trail_out: float32 [1024, 32768], P('cols', 'rows')
The draws below stay inside these ranges and needn't reach their ends.
Inputs may be any that keep to these rules, and one draw needn't show every extreme that they name: `panel_shift`: among the 64 panel and 256 trailing PSFs held by one index of cols, at most 40 have the same value of shift // 32, and exactly 40 share some value. `trail_shift`: as for panel_shift, over the same PSFs of one index of cols.
All inputs are finite; a program needn't handle non-finite values.
Results may differ from the reference program's by a relative error of at most 0.0003.
Values sent between devices are 32-bit elements; how exact they have to be, the bound alone decides.
A program may use at most 64 MiB of HBM per device.

```python
import math
import jax
import jax.numpy as jnp
from jax import lax

PANEL = 256
TRAIL = 1024
BW = 128
BLK_DEV = 32
NBLK = 256
NPIX = 32768
ROWGROUPS = 8
COLGROUPS = 4
PCOLS = 64
CW = 320
CAP = 40


def shift_table(key):
    base_key = jax.random.fold_in(key, 7)
    key_heavy, key_order, key_within = jax.random.split(base_key, 3)
    positions = jnp.arange(CW, dtype=jnp.int32)
    offsets = jnp.where(positions < CAP, 0, 1 + (positions - CAP) % (ROWGROUPS - 1))
    heavy = jax.random.randint(key_heavy, (COLGROUPS, 1), 0, ROWGROUPS)
    hops = (heavy + offsets[None, :]) % ROWGROUPS
    scores = jax.random.randint(key_order, (COLGROUPS, CW), 0, 1 << 20) * CW + positions[None, :]
    order = jnp.argsort(scores, axis=1)
    hops = jnp.take_along_axis(hops, order, axis=1)
    within = jax.random.randint(key_within, (COLGROUPS, CW), 0, BLK_DEV)
    table = (hops * BLK_DEV + within).astype(jnp.int32)
    return (table[:, :PCOLS].reshape(PANEL), table[:, PCOLS:].reshape(TRAIL))


def fresh_noise(key, salt, count):
    sub_key = jax.random.fold_in(key, salt)
    return jax.random.normal(sub_key, (count, NPIX), jnp.float32)


def row_scale(key):
    sub_key = jax.random.fold_in(key, 29)
    ramp = jnp.arange(NPIX, dtype=jnp.float32) / (NPIX - 1)
    rough = jnp.exp(jax.random.uniform(sub_key, (NPIX,), jnp.float32, math.log(0.5), math.log(2.0)))
    return rough * (1.0 + 2.0 * ramp)


def column_scale(key, salt, count):
    sub_key = jax.random.fold_in(key, salt)
    return jnp.exp(jax.random.uniform(sub_key, (count,), jnp.float32, math.log(0.3), math.log(3.0)))


def finish(key, fields, salt, shifts):
    count = fields.shape[0]
    values = fields * row_scale(key)[None, :] * column_scale(key, salt, count)[:, None]
    block_view = values.reshape(count, NBLK, BW)
    positions = jnp.arange(NBLK, dtype=jnp.int32)
    source_idx = (positions[None, :] + shifts[:, None]) % NBLK
    raw = jnp.take_along_axis(block_view, source_idx[:, :, None], axis=1)
    return raw.reshape(count, NPIX)


def draw_panel_shift(key, part):
    return shift_table(key)[0]


def draw_trail_shift(key, part):
    return shift_table(key)[1]


def draw_raw_panel(key, part):
    noise = fresh_noise(key, 11, PANEL + 1)
    fields = noise[1:] + 0.6 * noise[:-1]
    return finish(key, fields, 21, shift_table(key)[0])


def draw_raw_trail(key, part):
    noise = fresh_noise(key, 11, PANEL + 1)
    own_noise = fresh_noise(key, 13, TRAIL + 1)
    partner = 1 + jnp.arange(TRAIL, dtype=jnp.int32) % PANEL
    fields = own_noise[1:] + 0.6 * own_noise[:-1] + 0.8 * noise[partner]
    return finish(key, fields, 23, shift_table(key)[1])


def setup_inputs(seed: int = 0) -> dict:
    key_list = jax.random.split(jax.random.key(seed), 5)
    return {
        "raw_panel": draw_raw_panel(jax.random.fold_in(key_list[4], 71), 0),
        "raw_trail": draw_raw_trail(jax.random.fold_in(key_list[4], 71), 0),
        "panel_shift": draw_panel_shift(jax.random.fold_in(key_list[4], 71), 0),
        "trail_shift": draw_trail_shift(jax.random.fold_in(key_list[4], 71), 0),
    }


def register(raw_rows, shifts):
    count = raw_rows.shape[0]
    block_view = raw_rows.reshape(count, NBLK, BW)
    positions = jnp.arange(NBLK, dtype=jnp.int32)
    source_idx = ((positions[None, :] - shifts[:, None].astype(jnp.int32)) % NBLK).astype(jnp.int32)
    moved = jnp.take_along_axis(block_view, source_idx[:, :, None], axis=1)
    return moved.reshape(count, NPIX)

def reference(raw_panel, raw_trail, panel_shift, trail_shift):
    highest = lax.Precision.HIGHEST
    reg_panel = register(raw_panel, panel_shift)
    reg_trail = register(raw_trail, trail_shift)
    q_factor, r_upper = jnp.linalg.qr(reg_panel.T)
    flips = jnp.where(jnp.diagonal(r_upper) < 0, -1.0, 1.0).astype(r_upper.dtype)
    r_full = r_upper * flips[:, None]
    basis_t = (q_factor * flips[None, :]).T
    coupling_full = jnp.dot(basis_t, reg_trail.T, precision=highest)
    trail_out = reg_trail - jnp.dot(coupling_full.T, basis_t, precision=highest)
    root = math.sqrt(NPIX)
    return (r_full / root, coupling_full / root, basis_t * root, trail_out)
```

```python
import functools
import math

import jax
import jax.numpy as jnp
from jax import lax
from jax.experimental import pallas as pl
from jax.experimental.pallas import tpu as pltpu
from jax.sharding import PartitionSpec as P

BW = 128


def roll_kernel(n, count, blocks, shift_ref, in_hbm, out_ref, ring, sems):
    copies = []
    for i in range(n + 1):
        copies.append(
            pltpu.make_async_copy(
                in_hbm.at[i % n], ring.at[:, pl.ds(i * blocks, blocks)], sems.at[i]
            )
        )
    for copy in copies:
        copy.start()
    for copy in copies:
        copy.wait()
    total = n * blocks

    def one(k, carry):
        shift = shift_ref[k]
        for j in range(n):
            start = lax.rem(j * blocks - shift + total, total)
            out_ref[j, k] = ring[k, pl.ds(start, blocks), :]
        return carry

    lax.fori_loop(0, count, one, 0)


def roll_rows(whole, shifts):
    n, count, blocks, _ = whole.shape
    return pl.pallas_call(
        functools.partial(roll_kernel, n, count, blocks),
        out_shape=jax.ShapeDtypeStruct(whole.shape, whole.dtype),
        in_specs=[
            pl.BlockSpec(memory_space=pltpu.SMEM),
            pl.BlockSpec(memory_space=pl.ANY),
        ],
        out_specs=pl.BlockSpec(memory_space=pltpu.VMEM),
        scratch_shapes=[
            pltpu.VMEM((count, (n + 1) * blocks, BW), jnp.float32),
            pltpu.SemaphoreType.DMA((n + 1,)),
        ],
        cost_estimate=pl.CostEstimate(
            flops=0, bytes_accessed=2 * whole.size * 4, transcendentals=0
        ),
    )(shifts, whole)


def register(raw, shifts, n, my_row):
    rows, pixels = raw.shape
    blocks = pixels // BW
    padded = -(-rows // n) * n
    if padded != rows:
        raw = jnp.pad(raw, ((0, padded - rows), (0, 0)))
        shifts = jnp.pad(shifts, (0, padded - rows))
    count = padded // n
    outgoing = raw.reshape(n, count, blocks, BW)
    whole = lax.all_to_all(outgoing, "rows", split_axis=0, concat_axis=0, tiled=True)
    mine = lax.dynamic_slice_in_dim(shifts, my_row * count, count, 0)
    moved = roll_rows(whole, mine)
    back = lax.all_to_all(moved, "rows", split_axis=0, concat_axis=0, tiled=True)
    return back.reshape(padded, pixels)[:rows]


def inner_rows(left, right, precision):
    return lax.dot_general(
        left,
        right,
        (((1,), (1,)), ((), ())),
        precision=precision,
        preferred_element_type=jnp.float32,
    )


def on_device(raw_panel, raw_trail, panel_shift, trail_shift):
    pcols = raw_panel.shape[0]
    pixels = raw_panel.shape[1]
    n = lax.axis_size("rows")
    my_row = lax.axis_index("rows")
    reg_panel = register(raw_panel, panel_shift, n, my_row)
    reg_trail = register(raw_trail, trail_shift, n, my_row)
    full_panel = lax.all_gather(reg_panel, "cols", axis=0, tiled=True)
    gram = lax.psum(inner_rows(full_panel, full_panel, lax.Precision.HIGHEST), "rows")
    lower = jnp.linalg.cholesky(gram)
    eye = jnp.eye(lower.shape[0], dtype=jnp.float32)
    inverse = lax.linalg.triangular_solve(lower, eye, left_side=True, lower=True)
    basis_t = jnp.dot(
        inverse, full_panel, precision=lax.Precision.HIGH, preferred_element_type=jnp.float32
    )
    coupling = lax.psum(inner_rows(basis_t, reg_trail, lax.Precision.HIGH), "rows")
    removed = lax.dot_general(
        coupling,
        basis_t,
        (((0,), (0,)), ((), ())),
        precision=lax.Precision.HIGH,
        preferred_element_type=jnp.float32,
    )
    trail_out = reg_trail - removed
    root = math.sqrt(pixels * n)
    own_basis = lax.dynamic_slice_in_dim(basis_t, lax.axis_index("cols") * pcols, pcols, 0)
    return (lower.T / root, coupling / root, own_basis * root, trail_out)


def solution(mesh):
    placed = (P("cols", "rows"), P("cols", "rows"), P("cols"), P("cols"))
    return jax.shard_map(
        on_device,
        mesh=mesh,
        in_specs=placed,
        out_specs=(P(), P(None, "cols"), P("cols", "rows"), P("cols", "rows")),
        check_vma=False,
    )
```

```python
import functools
import math

import jax
import jax.numpy as jnp
from jax import lax
from jax.experimental import pallas as pl
from jax.experimental.pallas import tpu as pltpu
from jax.sharding import PartitionSpec as P

BW = 128
MESH = pl.DeviceIdType.MESH


def roll_kernel(n, count, blocks, shift_ref, in_hbm, out_ref, ring, sems):
    copies = []
    for i in range(n + 1):
        copies.append(
            pltpu.make_async_copy(
                in_hbm.at[i % n], ring.at[:, pl.ds(i * blocks, blocks)], sems.at[i]
            )
        )
    for copy in copies:
        copy.start()
    for copy in copies:
        copy.wait()
    total = n * blocks

    def one(k, carry):
        shift = shift_ref[k]
        for j in range(n):
            start = lax.rem(j * blocks - shift + total, total)
            out_ref[j, k] = ring[k, pl.ds(start, blocks), :]
        return carry

    lax.fori_loop(0, count, one, 0)


def roll_rows(whole, shifts):
    n, count, blocks, _ = whole.shape
    return pl.pallas_call(
        functools.partial(roll_kernel, n, count, blocks),
        out_shape=jax.ShapeDtypeStruct(whole.shape, whole.dtype),
        in_specs=[
            pl.BlockSpec(memory_space=pltpu.SMEM),
            pl.BlockSpec(memory_space=pl.ANY),
        ],
        out_specs=pl.BlockSpec(memory_space=pltpu.VMEM),
        scratch_shapes=[
            pltpu.VMEM((count, (n + 1) * blocks, BW), jnp.float32),
            pltpu.SemaphoreType.DMA((n + 1,)),
        ],
        cost_estimate=pl.CostEstimate(
            flops=0, bytes_accessed=2 * whole.size * 4, transcendentals=0
        ),
    )(shifts, whole)


def register(raw, shifts, n, my_row):
    rows, pixels = raw.shape
    blocks = pixels // BW
    padded = -(-rows // n) * n
    if padded != rows:
        raw = jnp.pad(raw, ((0, padded - rows), (0, 0)))
        shifts = jnp.pad(shifts, (0, padded - rows))
    count = padded // n
    outgoing = raw.reshape(n, count, blocks, BW)
    whole = lax.all_to_all(outgoing, "rows", split_axis=0, concat_axis=0, tiled=True)
    mine = lax.dynamic_slice_in_dim(shifts, my_row * count, count, 0)
    moved = roll_rows(whole, mine)
    back = lax.all_to_all(moved, "rows", split_axis=0, concat_axis=0, tiled=True)
    return back.reshape(padded, pixels)[:rows]


def inner_rows(left, right, precision):
    return lax.dot_general(
        left,
        right,
        (((1,), (1,)), ((), ())),
        precision=precision,
        preferred_element_type=jnp.float32,
    )


def sum_kernel(n, part_ref, out_ref, landed, send_one, recv_one, send_two, recv_two):
    me = lax.axis_index("rows")
    barrier = pltpu.get_barrier_semaphore()
    for d in range(1, n):
        pl.semaphore_signal(
            barrier, inc=1, device_id={"rows": lax.rem(me + d, n)}, device_id_type=MESH
        )
    pl.semaphore_wait(barrier, n - 1)
    scatter = []
    for d in range(1, n):
        to = lax.rem(me + d, n)
        copy = pltpu.make_async_remote_copy(
            src_ref=part_ref.at[to],
            dst_ref=landed.at[d - 1],
            send_sem=send_one.at[d - 1],
            recv_sem=recv_one.at[d - 1],
            device_id={"rows": to},
            device_id_type=MESH,
        )
        copy.start()
        scatter.append(copy)
    total = part_ref[me]
    for d in range(1, n):
        scatter[d - 1].wait_recv()
        total = total + landed[d - 1]
    out_ref[me] = total
    spread = []
    for d in range(1, n):
        to = lax.rem(me + d, n)
        copy = pltpu.make_async_remote_copy(
            src_ref=out_ref.at[me],
            dst_ref=out_ref.at[me],
            send_sem=send_two.at[d - 1],
            recv_sem=recv_two.at[d - 1],
            device_id={"rows": to},
            device_id_type=MESH,
        )
        copy.start()
        spread.append(copy)
    for copy in scatter:
        copy.wait_send()
    for copy in spread:
        copy.wait_recv()
    for copy in spread:
        copy.wait_send()


def sum_rows(part, n, ident):
    rows, columns = part.shape
    cut = (n, rows // n, columns)
    out = pl.pallas_call(
        functools.partial(sum_kernel, n),
        out_shape=jax.ShapeDtypeStruct(cut, jnp.float32),
        in_specs=[pl.BlockSpec(memory_space=pltpu.VMEM)],
        out_specs=pl.BlockSpec(memory_space=pltpu.VMEM),
        scratch_shapes=[pltpu.VMEM((n - 1,) + cut[1:], jnp.float32)]
        + [pltpu.SemaphoreType.DMA((n - 1,))] * 4,
        compiler_params=pltpu.CompilerParams(collective_id=ident, has_side_effects=True),
        cost_estimate=pl.CostEstimate(
            flops=0, bytes_accessed=16 * part.size * 4, transcendentals=0
        ),
    )(part.reshape(cut))
    return out.reshape(rows, columns)


def factor_kernel(size, tile, scale, gram_ref, upper_ref, inv_ref, aug, pair):
    grow = lax.broadcasted_iota(jnp.int32, (size, size), 0)
    gcol = lax.broadcasted_iota(jnp.int32, (size, size), 1)
    aug[:, 0:size] = gram_ref[...]
    aug[:, size : 2 * size] = jnp.where(grow == gcol, 1.0, 0.0)
    row = lax.broadcasted_iota(jnp.int32, (tile, 2 * tile), 0)
    col = lax.broadcasted_iota(jnp.int32, (tile, 2 * tile), 1)
    for lo in range(0, size, tile):
        hi = lo + tile
        pair[...] = jnp.where(col == row + tile, 1.0, 0.0)
        pair[:, 0:tile] = aug[lo:hi, lo:hi]
        w = pair[...]
        pivots = jnp.zeros((tile, 1), jnp.float32)
        for j in range(tile):
            base = j // 8 * 8
            live = w[base:, :]
            lead = w[j : j + 1, :]
            pivot = lead[:, j : j + 1]
            pivots = jnp.where(row[:, 0:1] == j, pivot, pivots)
            if j + 1 == tile:
                break
            mult = jnp.where(row[base:, 0:1] > j, live[:, j : j + 1], 0.0)
            live = live - mult * (lead / pivot)
            w = live if base == 0 else jnp.concatenate([w[:base], live], axis=0)
        pair[...] = w * (1.0 / jnp.sqrt(pivots))
        inverse = pair[:, tile : 2 * tile]
        lead_rows = lax.dot_general(
            inverse,
            aug[lo:hi, :],
            (((1,), (0,)), ((), ())),
            precision=lax.Precision.HIGHEST,
            preferred_element_type=jnp.float32,
        )
        keep = gcol[lo:hi] >= grow[lo:hi]
        upper = jnp.where(keep, lead_rows[:, 0:size], 0.0)
        upper_ref[lo:hi, :] = upper * scale
        inv_ref[lo:hi, :] = lead_rows[:, size : 2 * size]
        if hi < size:
            aug[...] = aug[...] - lax.dot_general(
                upper,
                lead_rows,
                (((0,), (0,)), ((), ())),
                precision=lax.Precision.HIGHEST,
                preferred_element_type=jnp.float32,
            )


def factor(gram, scale):
    size = gram.shape[0]
    tile = min(64, size)
    square = jax.ShapeDtypeStruct((size, size), jnp.float32)
    return pl.pallas_call(
        functools.partial(factor_kernel, size, tile, scale),
        out_shape=(square, square),
        in_specs=[pl.BlockSpec(memory_space=pltpu.VMEM)],
        out_specs=(pl.BlockSpec(memory_space=pltpu.VMEM),) * 2,
        scratch_shapes=[
            pltpu.VMEM((size, 2 * size), jnp.float32),
            pltpu.VMEM((tile, 2 * tile), jnp.float32),
        ],
        cost_estimate=pl.CostEstimate(
            flops=2 * size**3, bytes_accessed=60 * size * size * 4, transcendentals=0
        ),
    )(gram)


def on_device(raw_panel, raw_trail, panel_shift, trail_shift):
    pcols = raw_panel.shape[0]
    pixels = raw_panel.shape[1]
    n = lax.axis_size("rows")
    my_row = lax.axis_index("rows")
    root = math.sqrt(pixels * n)
    reg_panel = register(raw_panel, panel_shift, n, my_row)
    reg_trail = register(raw_trail, trail_shift, n, my_row)
    full_panel = lax.all_gather(reg_panel, "cols", axis=0, tiled=True)
    gram = sum_rows(inner_rows(full_panel, full_panel, lax.Precision.HIGHEST), n, 1)
    r_factor, inverse = factor(gram, 1.0 / root)
    cross = sum_rows(inner_rows(full_panel, reg_trail, lax.Precision.HIGH), n, 2)
    highest = lax.Precision.HIGHEST
    coupling = jnp.dot(inverse, cross, precision=highest, preferred_element_type=jnp.float32)
    weights = lax.dot_general(
        inverse,
        coupling,
        (((0,), (0,)), ((), ())),
        precision=highest,
        preferred_element_type=jnp.float32,
    )
    removed = lax.dot_general(
        weights,
        full_panel,
        (((0,), (0,)), ((), ())),
        precision=lax.Precision.HIGH,
        preferred_element_type=jnp.float32,
    )
    trail_out = reg_trail - removed
    own = lax.dynamic_slice_in_dim(inverse, lax.axis_index("cols") * pcols, pcols, 0)
    q_panel = jnp.dot(
        own * root, full_panel, precision=lax.Precision.HIGH, preferred_element_type=jnp.float32
    )
    return (r_factor, coupling / root, q_panel, trail_out)


def solution(mesh):
    placed = (P("cols", "rows"), P("cols", "rows"), P("cols"), P("cols"))
    return jax.shard_map(
        on_device,
        mesh=mesh,
        in_specs=placed,
        out_specs=(P(), P(None, "cols"), P("cols", "rows"), P("cols", "rows")),
        check_vma=False,
    )
```

```python
import functools
import math

import jax
import jax.numpy as jnp
from jax import lax
from jax.experimental import pallas as pl
from jax.experimental.pallas import tpu as pltpu
from jax.sharding import PartitionSpec as P

BW = 128
MESH = pl.DeviceIdType.MESH


def roll_rows(n, blocks, first, count, shift_ref, ring, moved):
    total = n * blocks

    def one(k, carry):
        shift = shift_ref[first + k]
        ring[k, pl.ds(total, blocks), :] = ring[k, pl.ds(0, blocks), :]
        for j in range(n):
            start = lax.rem(j * blocks - shift + total, total)
            moved[j, first + k] = ring[k, pl.ds(start, blocks), :]
        return carry

    lax.fori_loop(0, count, one, 0)


def exchange_kernel(
    n,
    depth,
    pieces,
    chunks,
    panel_shift,
    trail_shift,
    panel,
    trail,
    full,
    moved_t,
    ring_p,
    moved_p,
    p1_send,
    p1_recv,
    t1_send,
    t1_recv,
    p2_send,
    p2_recv,
    z_send,
    z_recv,
    local_sem,
    *rings,
):
    me = lax.axis_index("rows")
    z = lax.axis_index("cols")
    kp, blocks = panel.shape[1], panel.shape[2]
    kt = trail.shape[1]
    part = kt // chunks
    width = n // pieces * kp
    mine = pl.ds(pl.multiple_of(me * blocks, blocks), blocks)
    place = pl.ds(me * kp, kp)

    barrier = pltpu.get_barrier_semaphore()
    for d in range(1, n):
        pl.semaphore_signal(
            barrier, inc=1, device_id={"rows": lax.rem(me + d, n)}, device_id_type=MESH
        )

    @pl.when(z > 0)
    def _():
        pl.semaphore_signal(barrier, inc=1, device_id={"cols": z - 1}, device_id_type=MESH)

    @pl.when(z < depth - 1)
    def _():
        pl.semaphore_signal(barrier, inc=1, device_id={"cols": z + 1}, device_id_type=MESH)

    sides = jnp.where(z > 0, 1, 0) + jnp.where(z < depth - 1, 1, 0)
    pl.semaphore_wait(barrier, n - 1 + sides)

    def row_copy(src, dst, send, recv, to):
        return pltpu.make_async_remote_copy(
            src_ref=src,
            dst_ref=dst,
            send_sem=send,
            recv_sem=recv,
            device_id={"rows": to},
            device_id_type=MESH,
        )

    far = [lax.rem(me + d, n) for d in range(1, n)]
    p1 = [
        row_copy(panel.at[to], ring_p.at[:, mine], p1_send.at[i], p1_recv.at[i], to)
        for i, to in enumerate(far)
    ]
    own_p1 = pltpu.make_async_copy(panel.at[me], ring_p.at[:, mine], local_sem.at[0])
    t1, own_t1 = [], []
    for c in range(chunks):
        span = pl.ds(c * part, part)
        t1.append(
            [
                row_copy(
                    trail.at[to, span],
                    rings[c].at[:, mine],
                    t1_send.at[c, i],
                    t1_recv.at[c, i],
                    to,
                )
                for i, to in enumerate(far)
            ]
        )
        own_t1.append(
            pltpu.make_async_copy(
                trail.at[me, span], rings[c].at[:, mine], local_sem.at[2 + c]
            )
        )
    p2 = [
        row_copy(moved_p.at[to], full.at[z, place], p2_send.at[i], p2_recv.at[i], to)
        for i, to in enumerate(far)
    ]
    own_p2 = pltpu.make_async_copy(moved_p.at[me], full.at[z, place], local_sem.at[1])

    def line(side, d, q):
        step = 1 if side == 0 else -1
        origin = z - step * (d - 1)
        rows = pl.ds(q * width, width)
        return pltpu.make_async_remote_copy(
            src_ref=full.at[origin, rows],
            dst_ref=full.at[origin, rows],
            send_sem=z_send.at[side, d - 1, q],
            recv_sem=z_recv.at[side, d - 1, q],
            device_id={"cols": z + step},
            device_id_type=MESH,
        )

    def sends(side, d):
        if side == 0:
            return (z + 1 < depth) & (z - (d - 1) >= 0)
        return (z >= 1) & (z + (d - 1) < depth)

    def receives(side, d):
        return z - d >= 0 if side == 0 else z + d < depth

    def arrived(side, d, q):
        step = 1 if side == 0 else -1
        origin = z - step * d
        rows = pl.ds(q * width, width)
        return pltpu.make_async_remote_copy(
            src_ref=full.at[origin, rows],
            dst_ref=full.at[origin, rows],
            send_sem=z_send.at[side, d - 1, q],
            recv_sem=z_recv.at[side, d - 1, q],
            device_id={"cols": z - step},
            device_id_type=MESH,
        )

    own_p1.start()
    for copy in p1:
        copy.start()
    own_t1[0].start()
    for copy in t1[0]:
        copy.start()
    own_p1.wait()
    for copy in p1:
        copy.wait_recv()
    roll_rows(n, blocks, 0, kp, panel_shift, ring_p, moved_p)
    own_p2.start()
    for copy in p2:
        copy.start()
    for c in range(1, chunks):
        own_t1[c].start()
        for copy in t1[c]:
            copy.start()
    own_p2.wait()
    for copy in p2:
        copy.wait_recv()
    for q in range(pieces):
        for side in (0, 1):

            @pl.when(sends(side, 1))
            def _():
                line(side, 1, q).start()

    for c in range(chunks):
        if c == chunks - 1:
            for d in range(1, depth):
                for q in range(pieces):
                    for side in (0, 1):

                        @pl.when(receives(side, d))
                        def _():
                            arrived(side, d, q).wait_recv()

                        if d + 1 < depth:

                            @pl.when(sends(side, d + 1))
                            def _():
                                line(side, d + 1, q).start()

        own_t1[c].wait()
        for copy in t1[c]:
            copy.wait_recv()
        roll_rows(n, blocks, c * part, part, trail_shift, rings[c], moved_t)
    for copy in p1 + p2 + sum(t1, []):
        copy.wait_send()
    for d in range(1, depth):
        for q in range(pieces):
            for side in (0, 1):

                @pl.when(sends(side, d))
                def _():
                    line(side, d, q).wait_send()


def exchange(panel, trail, panel_shift, trail_shift, n, depth):
    _, kp, blocks, _ = panel.shape
    kt = trail.shape[1]
    pieces = 4 if n % 4 == 0 else 1
    chunks = 2 if kt % 2 == 0 else 1
    f32 = jnp.float32
    smem = pl.BlockSpec(memory_space=pltpu.SMEM)
    vmem = pl.BlockSpec(memory_space=pltpu.VMEM)
    hbm = pl.BlockSpec(memory_space=pl.ANY)
    dma = pltpu.SemaphoreType.DMA
    return pl.pallas_call(
        functools.partial(exchange_kernel, n, depth, pieces, chunks),
        out_shape=(
            jax.ShapeDtypeStruct((depth, n * kp, blocks, BW), f32),
            jax.ShapeDtypeStruct(trail.shape, f32),
        ),
        in_specs=[smem, smem, hbm, hbm],
        out_specs=(vmem, vmem),
        scratch_shapes=[
            pltpu.VMEM((kp, (n + 1) * blocks, BW), f32),
            pltpu.VMEM((n, kp, blocks, BW), f32),
            dma((n - 1,)),
            dma((n - 1,)),
            dma((chunks, n - 1)),
            dma((chunks, n - 1)),
            dma((n - 1,)),
            dma((n - 1,)),
            dma((2, max(depth - 1, 1), pieces)),
            dma((2, max(depth - 1, 1), pieces)),
            dma((2 + chunks,)),
        ]
        + [pltpu.VMEM((kt // chunks, (n + 1) * blocks, BW), f32)] * chunks,
        compiler_params=pltpu.CompilerParams(collective_id=3, has_side_effects=True),
        cost_estimate=pl.CostEstimate(
            flops=0, bytes_accessed=40 * trail.size * 4, transcendentals=0
        ),
    )(panel_shift, trail_shift, panel, trail)


def grouped(raw, shifts, n, my_row):
    rows, pixels = raw.shape
    padded = -(-rows // n) * n
    if padded != rows:
        raw = jnp.pad(raw, ((0, padded - rows), (0, 0)))
        shifts = jnp.pad(shifts, (0, padded - rows))
    count = padded // n
    mine = lax.dynamic_slice_in_dim(shifts, my_row * count, count, 0)
    return raw.reshape(n, count, pixels // BW, BW), mine


def inner_rows(left, right, precision):
    return lax.dot_general(
        left,
        right,
        (((1,), (1,)), ((), ())),
        precision=precision,
        preferred_element_type=jnp.float32,
    )


def sum_kernel(n, part_ref, out_ref, landed, send_one, recv_one, send_two, recv_two):
    me = lax.axis_index("rows")
    barrier = pltpu.get_barrier_semaphore()
    for d in range(1, n):
        pl.semaphore_signal(
            barrier, inc=1, device_id={"rows": lax.rem(me + d, n)}, device_id_type=MESH
        )
    pl.semaphore_wait(barrier, n - 1)
    scatter = []
    for d in range(1, n):
        to = lax.rem(me + d, n)
        copy = pltpu.make_async_remote_copy(
            src_ref=part_ref.at[to],
            dst_ref=landed.at[d - 1],
            send_sem=send_one.at[d - 1],
            recv_sem=recv_one.at[d - 1],
            device_id={"rows": to},
            device_id_type=MESH,
        )
        copy.start()
        scatter.append(copy)
    total = part_ref[me]
    for d in range(1, n):
        scatter[d - 1].wait_recv()
        total = total + landed[d - 1]
    out_ref[me] = total
    spread = []
    for d in range(1, n):
        to = lax.rem(me + d, n)
        copy = pltpu.make_async_remote_copy(
            src_ref=out_ref.at[me],
            dst_ref=out_ref.at[me],
            send_sem=send_two.at[d - 1],
            recv_sem=recv_two.at[d - 1],
            device_id={"rows": to},
            device_id_type=MESH,
        )
        copy.start()
        spread.append(copy)
    for copy in scatter:
        copy.wait_send()
    for copy in spread:
        copy.wait_recv()
    for copy in spread:
        copy.wait_send()


def sum_rows(part, n, ident):
    rows, columns = part.shape
    cut = (n, rows // n, columns)
    out = pl.pallas_call(
        functools.partial(sum_kernel, n),
        out_shape=jax.ShapeDtypeStruct(cut, jnp.float32),
        in_specs=[pl.BlockSpec(memory_space=pltpu.VMEM)],
        out_specs=pl.BlockSpec(memory_space=pltpu.VMEM),
        scratch_shapes=[pltpu.VMEM((n - 1,) + cut[1:], jnp.float32)]
        + [pltpu.SemaphoreType.DMA((n - 1,))] * 4,
        compiler_params=pltpu.CompilerParams(collective_id=ident, has_side_effects=True),
        cost_estimate=pl.CostEstimate(
            flops=0, bytes_accessed=16 * part.size * 4, transcendentals=0
        ),
    )(part.reshape(cut))
    return out.reshape(rows, columns)


def factor_kernel(size, tile, scale, gram_ref, upper_ref, inv_ref, aug, pair):
    grow = lax.broadcasted_iota(jnp.int32, (size, size), 0)
    gcol = lax.broadcasted_iota(jnp.int32, (size, size), 1)
    aug[:, 0:size] = gram_ref[...]
    aug[:, size : 2 * size] = jnp.where(grow == gcol, 1.0, 0.0)
    row = lax.broadcasted_iota(jnp.int32, (tile, 2 * tile), 0)
    col = lax.broadcasted_iota(jnp.int32, (tile, 2 * tile), 1)
    for lo in range(0, size, tile):
        hi = lo + tile
        pair[...] = jnp.where(col == row + tile, 1.0, 0.0)
        pair[:, 0:tile] = aug[lo:hi, lo:hi]
        w = pair[...]
        pivots = jnp.zeros((tile, 1), jnp.float32)
        for j in range(tile):
            base = j // 8 * 8
            live = w[base:, :]
            lead = w[j : j + 1, :]
            pivot = lead[:, j : j + 1]
            pivots = jnp.where(row[:, 0:1] == j, pivot, pivots)
            if j + 1 == tile:
                break
            mult = jnp.where(row[base:, 0:1] > j, live[:, j : j + 1], 0.0)
            live = live - mult * (lead / pivot)
            w = live if base == 0 else jnp.concatenate([w[:base], live], axis=0)
        pair[...] = w * (1.0 / jnp.sqrt(pivots))
        inverse = pair[:, tile : 2 * tile]
        lead_rows = lax.dot_general(
            inverse,
            aug[lo:hi, :],
            (((1,), (0,)), ((), ())),
            precision=lax.Precision.HIGHEST,
            preferred_element_type=jnp.float32,
        )
        keep = gcol[lo:hi] >= grow[lo:hi]
        upper = jnp.where(keep, lead_rows[:, 0:size], 0.0)
        upper_ref[lo:hi, :] = upper * scale
        inv_ref[lo:hi, :] = lead_rows[:, size : 2 * size]
        if hi < size:
            aug[...] = aug[...] - lax.dot_general(
                upper,
                lead_rows,
                (((0,), (0,)), ((), ())),
                precision=lax.Precision.HIGHEST,
                preferred_element_type=jnp.float32,
            )


def factor(gram, scale):
    size = gram.shape[0]
    tile = min(64, size)
    square = jax.ShapeDtypeStruct((size, size), jnp.float32)
    return pl.pallas_call(
        functools.partial(factor_kernel, size, tile, scale),
        out_shape=(square, square),
        in_specs=[pl.BlockSpec(memory_space=pltpu.VMEM)],
        out_specs=(pl.BlockSpec(memory_space=pltpu.VMEM),) * 2,
        scratch_shapes=[
            pltpu.VMEM((size, 2 * size), jnp.float32),
            pltpu.VMEM((tile, 2 * tile), jnp.float32),
        ],
        cost_estimate=pl.CostEstimate(
            flops=2 * size**3, bytes_accessed=60 * size * size * 4, transcendentals=0
        ),
    )(gram)


def on_device(raw_panel, raw_trail, panel_shift, trail_shift):
    pcols = raw_panel.shape[0]
    pixels = raw_panel.shape[1]
    n = lax.axis_size("rows")
    my_row = lax.axis_index("rows")
    root = math.sqrt(pixels * n)
    depth = lax.axis_size("cols")
    trows = raw_trail.shape[0]
    panel, panel_mine = grouped(raw_panel, panel_shift, n, my_row)
    trail, trail_mine = grouped(raw_trail, trail_shift, n, my_row)
    full, moved = exchange(panel, trail, panel_mine, trail_mine, n, depth)
    full_panel = full.reshape(depth, -1, pixels)[:, :pcols].reshape(depth * pcols, pixels)
    back = lax.all_to_all(moved, "rows", split_axis=0, concat_axis=0, tiled=True)
    reg_trail = back.reshape(-1, pixels)[:trows]
    gram = sum_rows(inner_rows(full_panel, full_panel, lax.Precision.HIGHEST), n, 1)
    r_factor, inverse = factor(gram, 1.0 / root)
    cross = sum_rows(inner_rows(full_panel, reg_trail, lax.Precision.HIGH), n, 2)
    highest = lax.Precision.HIGHEST
    coupling = jnp.dot(inverse, cross, precision=highest, preferred_element_type=jnp.float32)
    weights = lax.dot_general(
        inverse,
        coupling,
        (((0,), (0,)), ((), ())),
        precision=highest,
        preferred_element_type=jnp.float32,
    )
    removed = lax.dot_general(
        weights,
        full_panel,
        (((0,), (0,)), ((), ())),
        precision=lax.Precision.HIGH,
        preferred_element_type=jnp.float32,
    )
    trail_out = reg_trail - removed
    own = lax.dynamic_slice_in_dim(inverse, lax.axis_index("cols") * pcols, pcols, 0)
    q_panel = jnp.dot(
        own * root, full_panel, precision=lax.Precision.HIGH, preferred_element_type=jnp.float32
    )
    return (r_factor, coupling / root, q_panel, trail_out)


def solution(mesh):
    placed = (P("cols", "rows"), P("cols", "rows"), P("cols"), P("cols"))
    return jax.shard_map(
        on_device,
        mesh=mesh,
        in_specs=placed,
        out_specs=(P(), P(None, "cols"), P("cols", "rows"), P("cols", "rows")),
        check_vma=False,
    )
```

```python
import functools
import math

import jax
import jax.numpy as jnp
from jax import lax
from jax.experimental import pallas as pl
from jax.experimental.pallas import tpu as pltpu
from jax.sharding import PartitionSpec as P

BW = 128
MESH = pl.DeviceIdType.MESH


def roll_rows(n, blocks, first, count, shift_ref, ring, moved):
    total = n * blocks

    def one(k, carry):
        shift = shift_ref[first + k]
        ring[k, pl.ds(total, blocks), :] = ring[k, pl.ds(0, blocks), :]
        for j in range(n):
            start = lax.rem(j * blocks - shift + total, total)
            moved[j, k] = ring[k, pl.ds(start, blocks), :]
        return carry

    lax.fori_loop(0, count, one, 0)


def exchange_kernel(
    n,
    depth,
    pieces,
    chunks,
    panel_shift,
    trail_shift,
    panel,
    trail,
    full,
    back,
    moved_b,
    ring_p,
    moved_p,
    moved_a,
    p1_send,
    p1_recv,
    t1_send,
    t1_recv,
    p2_send,
    p2_recv,
    t2_send,
    t2_recv,
    z_send,
    z_recv,
    local_sem,
    *rings,
):
    me = lax.axis_index("rows")
    z = lax.axis_index("cols")
    kp, blocks = panel.shape[1], panel.shape[2]
    kt = trail.shape[1]
    part = kt // chunks
    width = n // pieces * kp
    mine = pl.ds(pl.multiple_of(me * blocks, blocks), blocks)
    place = pl.ds(me * kp, kp)

    barrier = pltpu.get_barrier_semaphore()
    for d in range(1, n):
        pl.semaphore_signal(
            barrier, inc=1, device_id={"rows": lax.rem(me + d, n)}, device_id_type=MESH
        )

    @pl.when(z > 0)
    def _():
        pl.semaphore_signal(barrier, inc=1, device_id={"cols": z - 1}, device_id_type=MESH)

    @pl.when(z < depth - 1)
    def _():
        pl.semaphore_signal(barrier, inc=1, device_id={"cols": z + 1}, device_id_type=MESH)

    sides = jnp.where(z > 0, 1, 0) + jnp.where(z < depth - 1, 1, 0)
    pl.semaphore_wait(barrier, n - 1 + sides)

    def row_copy(src, dst, send, recv, to):
        return pltpu.make_async_remote_copy(
            src_ref=src,
            dst_ref=dst,
            send_sem=send,
            recv_sem=recv,
            device_id={"rows": to},
            device_id_type=MESH,
        )

    far = [lax.rem(me + d, n) for d in range(1, n)]
    p1 = [
        row_copy(panel.at[to], ring_p.at[:, mine], p1_send.at[i], p1_recv.at[i], to)
        for i, to in enumerate(far)
    ]
    own_p1 = pltpu.make_async_copy(panel.at[me], ring_p.at[:, mine], local_sem.at[0])
    t1, own_t1 = [], []
    for c in range(chunks):
        span = pl.ds(c * part, part)
        t1.append(
            [
                row_copy(
                    trail.at[to, span],
                    rings[c].at[:, mine],
                    t1_send.at[c, i],
                    t1_recv.at[c, i],
                    to,
                )
                for i, to in enumerate(far)
            ]
        )
        own_t1.append(
            pltpu.make_async_copy(
                trail.at[me, span], rings[c].at[:, mine], local_sem.at[2 + c]
            )
        )
    p2 = [
        row_copy(moved_p.at[to], full.at[z, place], p2_send.at[i], p2_recv.at[i], to)
        for i, to in enumerate(far)
    ]
    t2 = [
        row_copy(moved_a.at[to], back.at[me], t2_send.at[i], t2_recv.at[i], to)
        for i, to in enumerate(far)
    ]
    own_t2 = pltpu.make_async_copy(moved_a.at[me], back.at[me], local_sem.at[2 + chunks])
    own_p2 = pltpu.make_async_copy(moved_p.at[me], full.at[z, place], local_sem.at[1])

    def line(side, d, q):
        step = 1 if side == 0 else -1
        origin = z - step * (d - 1)
        rows = pl.ds(q * width, width)
        return pltpu.make_async_remote_copy(
            src_ref=full.at[origin, rows],
            dst_ref=full.at[origin, rows],
            send_sem=z_send.at[side, d - 1, q],
            recv_sem=z_recv.at[side, d - 1, q],
            device_id={"cols": z + step},
            device_id_type=MESH,
        )

    def sends(side, d):
        if side == 0:
            return (z + 1 < depth) & (z - (d - 1) >= 0)
        return (z >= 1) & (z + (d - 1) < depth)

    def receives(side, d):
        return z - d >= 0 if side == 0 else z + d < depth

    def arrived(side, d, q):
        step = 1 if side == 0 else -1
        origin = z - step * d
        rows = pl.ds(q * width, width)
        return pltpu.make_async_remote_copy(
            src_ref=full.at[origin, rows],
            dst_ref=full.at[origin, rows],
            send_sem=z_send.at[side, d - 1, q],
            recv_sem=z_recv.at[side, d - 1, q],
            device_id={"cols": z - step},
            device_id_type=MESH,
        )

    def forward(d):
        for q in range(pieces):
            for side in (0, 1):

                @pl.when(receives(side, d))
                def _():
                    arrived(side, d, q).wait_recv()

                if d + 1 < depth:

                    @pl.when(sends(side, d + 1))
                    def _():
                        line(side, d + 1, q).start()

    own_p1.start()
    for copy in p1:
        copy.start()
    own_p1.wait()
    for copy in p1:
        copy.wait_recv()
    roll_rows(n, blocks, 0, kp, panel_shift, ring_p, moved_p)
    own_p2.start()
    for copy in p2:
        copy.start()
    for c in range(chunks):
        own_t1[c].start()
        for copy in t1[c]:
            copy.start()
    own_p2.wait()
    for copy in p2:
        copy.wait_recv()
    for q in range(pieces):
        for side in (0, 1):

            @pl.when(sends(side, 1))
            def _():
                line(side, 1, q).start()

    forward(1)
    own_t1[0].wait()
    for copy in t1[0]:
        copy.wait_recv()
    roll_rows(n, blocks, 0, part, trail_shift, rings[0], moved_a)
    own_t2.start()
    for copy in t2:
        copy.start()
    if depth > 2:
        forward(2)
    own_t1[1].wait()
    for copy in t1[1]:
        copy.wait_recv()
    roll_rows(n, blocks, part, part, trail_shift, rings[1], moved_b)
    for d in range(3, depth):
        forward(d)
    own_t2.wait()
    for copy in t2:
        copy.wait_recv()
    for copy in p1 + p2 + t1[0] + t1[1] + t2:
        copy.wait_send()
    for d in range(1, depth):
        for q in range(pieces):
            for side in (0, 1):

                @pl.when(sends(side, d))
                def _():
                    line(side, d, q).wait_send()


def exchange(panel, trail, panel_shift, trail_shift, n, depth):
    _, kp, blocks, _ = panel.shape
    kt = trail.shape[1]
    pieces = 4 if n % 4 == 0 else 1
    chunks = 2
    half = jax.ShapeDtypeStruct((n, kt // 2, blocks, BW), jnp.float32)
    f32 = jnp.float32
    smem = pl.BlockSpec(memory_space=pltpu.SMEM)
    vmem = pl.BlockSpec(memory_space=pltpu.VMEM)
    hbm = pl.BlockSpec(memory_space=pl.ANY)
    dma = pltpu.SemaphoreType.DMA
    return pl.pallas_call(
        functools.partial(exchange_kernel, n, depth, pieces, chunks),
        out_shape=(
            jax.ShapeDtypeStruct((depth, n * kp, blocks, BW), f32),
            half,
            half,
        ),
        in_specs=[smem, smem, hbm, hbm],
        out_specs=(vmem,) * 3,
        scratch_shapes=[
            pltpu.VMEM((kp, (n + 1) * blocks, BW), f32),
            pltpu.VMEM((n, kp, blocks, BW), f32),
            pltpu.VMEM(half.shape, f32),
            dma((n - 1,)),
            dma((n - 1,)),
            dma((chunks, n - 1)),
            dma((chunks, n - 1)),
            dma((n - 1,)),
            dma((n - 1,)),
            dma((n - 1,)),
            dma((n - 1,)),
            dma((2, max(depth - 1, 1), pieces)),
            dma((2, max(depth - 1, 1), pieces)),
            dma((3 + chunks,)),
        ]
        + [pltpu.VMEM((kt // chunks, (n + 1) * blocks, BW), f32)] * chunks,
        compiler_params=pltpu.CompilerParams(collective_id=3, has_side_effects=True),
        cost_estimate=pl.CostEstimate(
            flops=0, bytes_accessed=40 * trail.size * 4, transcendentals=0
        ),
    )(panel_shift, trail_shift, panel, trail)


def grouped(raw, shifts, n, my_row, unit):
    rows, pixels = raw.shape
    padded = -(-rows // (n * unit)) * n * unit
    if padded != rows:
        raw = jnp.pad(raw, ((0, padded - rows), (0, 0)))
        shifts = jnp.pad(shifts, (0, padded - rows))
    count = padded // n
    mine = lax.dynamic_slice_in_dim(shifts, my_row * count, count, 0)
    return raw.reshape(n, count, pixels // BW, BW), mine


def inner_rows(left, right, precision):
    return lax.dot_general(
        left,
        right,
        (((1,), (1,)), ((), ())),
        precision=precision,
        preferred_element_type=jnp.float32,
    )


def sum_kernel(n, part_ref, out_ref, landed, send_one, recv_one, send_two, recv_two):
    me = lax.axis_index("rows")
    barrier = pltpu.get_barrier_semaphore()
    for d in range(1, n):
        pl.semaphore_signal(
            barrier, inc=1, device_id={"rows": lax.rem(me + d, n)}, device_id_type=MESH
        )
    pl.semaphore_wait(barrier, n - 1)
    scatter = []
    for d in range(1, n):
        to = lax.rem(me + d, n)
        copy = pltpu.make_async_remote_copy(
            src_ref=part_ref.at[to],
            dst_ref=landed.at[d - 1],
            send_sem=send_one.at[d - 1],
            recv_sem=recv_one.at[d - 1],
            device_id={"rows": to},
            device_id_type=MESH,
        )
        copy.start()
        scatter.append(copy)
    total = part_ref[me]
    for d in range(1, n):
        scatter[d - 1].wait_recv()
        total = total + landed[d - 1]
    out_ref[me] = total
    spread = []
    for d in range(1, n):
        to = lax.rem(me + d, n)
        copy = pltpu.make_async_remote_copy(
            src_ref=out_ref.at[me],
            dst_ref=out_ref.at[me],
            send_sem=send_two.at[d - 1],
            recv_sem=recv_two.at[d - 1],
            device_id={"rows": to},
            device_id_type=MESH,
        )
        copy.start()
        spread.append(copy)
    for copy in scatter:
        copy.wait_send()
    for copy in spread:
        copy.wait_recv()
    for copy in spread:
        copy.wait_send()


def sum_rows(part, n, ident):
    rows, columns = part.shape
    cut = (n, rows // n, columns)
    out = pl.pallas_call(
        functools.partial(sum_kernel, n),
        out_shape=jax.ShapeDtypeStruct(cut, jnp.float32),
        in_specs=[pl.BlockSpec(memory_space=pltpu.VMEM)],
        out_specs=pl.BlockSpec(memory_space=pltpu.VMEM),
        scratch_shapes=[pltpu.VMEM((n - 1,) + cut[1:], jnp.float32)]
        + [pltpu.SemaphoreType.DMA((n - 1,))] * 4,
        compiler_params=pltpu.CompilerParams(collective_id=ident, has_side_effects=True),
        cost_estimate=pl.CostEstimate(
            flops=0, bytes_accessed=16 * part.size * 4, transcendentals=0
        ),
    )(part.reshape(cut))
    return out.reshape(rows, columns)


def factor_kernel(size, tile, scale, gram_ref, upper_ref, inv_ref, aug, pair):
    grow = lax.broadcasted_iota(jnp.int32, (size, size), 0)
    gcol = lax.broadcasted_iota(jnp.int32, (size, size), 1)
    aug[:, 0:size] = gram_ref[...]
    aug[:, size : 2 * size] = jnp.where(grow == gcol, 1.0, 0.0)
    row = lax.broadcasted_iota(jnp.int32, (tile, 2 * tile), 0)
    col = lax.broadcasted_iota(jnp.int32, (tile, 2 * tile), 1)
    for lo in range(0, size, tile):
        hi = lo + tile
        pair[...] = jnp.where(col == row + tile, 1.0, 0.0)
        pair[:, 0:tile] = aug[lo:hi, lo:hi]
        w = pair[...]
        pivots = jnp.zeros((tile, 1), jnp.float32)
        for j in range(tile):
            base = j // 8 * 8
            live = w[base:, :]
            lead = w[j : j + 1, :]
            pivot = lead[:, j : j + 1]
            pivots = jnp.where(row[:, 0:1] == j, pivot, pivots)
            if j + 1 == tile:
                break
            mult = jnp.where(row[base:, 0:1] > j, live[:, j : j + 1], 0.0)
            live = live - mult * (lead / pivot)
            w = live if base == 0 else jnp.concatenate([w[:base], live], axis=0)
        pair[...] = w * (1.0 / jnp.sqrt(pivots))
        inverse = pair[:, tile : 2 * tile]
        lead_rows = lax.dot_general(
            inverse,
            aug[lo:hi, :],
            (((1,), (0,)), ((), ())),
            precision=lax.Precision.HIGHEST,
            preferred_element_type=jnp.float32,
        )
        keep = gcol[lo:hi] >= grow[lo:hi]
        upper = jnp.where(keep, lead_rows[:, 0:size], 0.0)
        upper_ref[lo:hi, :] = upper * scale
        inv_ref[lo:hi, :] = lead_rows[:, size : 2 * size]
        if hi < size:
            aug[...] = aug[...] - lax.dot_general(
                upper,
                lead_rows,
                (((0,), (0,)), ((), ())),
                precision=lax.Precision.HIGHEST,
                preferred_element_type=jnp.float32,
            )


def factor(gram, scale):
    size = gram.shape[0]
    tile = min(64, size)
    square = jax.ShapeDtypeStruct((size, size), jnp.float32)
    return pl.pallas_call(
        functools.partial(factor_kernel, size, tile, scale),
        out_shape=(square, square),
        in_specs=[pl.BlockSpec(memory_space=pltpu.VMEM)],
        out_specs=(pl.BlockSpec(memory_space=pltpu.VMEM),) * 2,
        scratch_shapes=[
            pltpu.VMEM((size, 2 * size), jnp.float32),
            pltpu.VMEM((tile, 2 * tile), jnp.float32),
        ],
        cost_estimate=pl.CostEstimate(
            flops=2 * size**3, bytes_accessed=60 * size * size * 4, transcendentals=0
        ),
    )(gram)


def on_device(raw_panel, raw_trail, panel_shift, trail_shift):
    pcols = raw_panel.shape[0]
    pixels = raw_panel.shape[1]
    n = lax.axis_size("rows")
    my_row = lax.axis_index("rows")
    root = math.sqrt(pixels * n)
    depth = lax.axis_size("cols")
    trows = raw_trail.shape[0]
    panel, panel_mine = grouped(raw_panel, panel_shift, n, my_row, 1)
    trail, trail_mine = grouped(raw_trail, trail_shift, n, my_row, 2)
    full, front, moved = exchange(panel, trail, panel_mine, trail_mine, n, depth)
    full_panel = full.reshape(depth, -1, pixels)[:, :pcols].reshape(depth * pcols, pixels)
    full_panel = lax.optimization_barrier(full_panel)
    rest = lax.all_to_all(moved, "rows", split_axis=0, concat_axis=0, tiled=True)
    reg_trail = jnp.concatenate([front, rest], axis=1).reshape(-1, pixels)[:trows]
    reg_trail = lax.optimization_barrier(reg_trail)
    gram = sum_rows(inner_rows(full_panel, full_panel, lax.Precision.HIGHEST), n, 1)
    r_factor, inverse = factor(gram, 1.0 / root)
    cross = sum_rows(inner_rows(full_panel, reg_trail, lax.Precision.HIGH), n, 2)
    highest = lax.Precision.HIGHEST
    coupling = jnp.dot(inverse, cross, precision=highest, preferred_element_type=jnp.float32)
    weights = lax.dot_general(
        inverse,
        coupling,
        (((0,), (0,)), ((), ())),
        precision=highest,
        preferred_element_type=jnp.float32,
    )
    removed = lax.dot_general(
        weights,
        full_panel,
        (((0,), (0,)), ((), ())),
        precision=lax.Precision.HIGH,
        preferred_element_type=jnp.float32,
    )
    trail_out = reg_trail - removed
    own = lax.dynamic_slice_in_dim(inverse, lax.axis_index("cols") * pcols, pcols, 0)
    q_panel = jnp.dot(
        own * root, full_panel, precision=lax.Precision.HIGH, preferred_element_type=jnp.float32
    )
    return (r_factor, coupling / root, q_panel, trail_out)


def solution(mesh):
    placed = (P("cols", "rows"), P("cols", "rows"), P("cols"), P("cols"))
    return jax.shard_map(
        on_device,
        mesh=mesh,
        in_specs=placed,
        out_specs=(P(), P(None, "cols"), P("cols", "rows"), P("cols", "rows")),
        check_vma=False,
    )
```

```python
import functools
import math

import jax
import jax.numpy as jnp
from jax import lax
from jax.experimental import pallas as pl
from jax.experimental.pallas import tpu as pltpu
from jax.sharding import PartitionSpec as P

BW = 128
MESH = pl.DeviceIdType.MESH


def roll_rows(n, blocks, first, count, shift_ref, ring, moved):
    total = n * blocks

    def one(k, carry):
        shift = shift_ref[first + k]
        ring[k, pl.ds(total, blocks), :] = ring[k, pl.ds(0, blocks), :]
        for j in range(n):
            start = lax.rem(j * blocks - shift + total, total)
            moved[j, k] = ring[k, pl.ds(start, blocks), :]
        return carry

    lax.fori_loop(0, count, one, 0)


def exchange_kernel(
    n,
    depth,
    pieces,
    chunks,
    panel_shift,
    trail_shift,
    panel,
    trail,
    full,
    back,
    moved_b,
    ring_p,
    moved_p,
    moved_a,
    p1_send,
    p1_recv,
    t1_send,
    t1_recv,
    p2_send,
    p2_recv,
    t2_send,
    t2_recv,
    z_send,
    z_recv,
    local_sem,
    *rings,
):
    me = lax.axis_index("rows")
    z = lax.axis_index("cols")
    kp, blocks = panel.shape[1], panel.shape[2]
    kt = trail.shape[1]
    part = kt // chunks
    width = n // pieces * kp
    mine = pl.ds(pl.multiple_of(me * blocks, blocks), blocks)
    place = pl.ds(me * kp, kp)

    barrier = pltpu.get_barrier_semaphore()
    for d in range(1, n):
        pl.semaphore_signal(
            barrier, inc=1, device_id={"rows": lax.rem(me + d, n)}, device_id_type=MESH
        )

    @pl.when(z > 0)
    def _():
        pl.semaphore_signal(barrier, inc=1, device_id={"cols": z - 1}, device_id_type=MESH)

    @pl.when(z < depth - 1)
    def _():
        pl.semaphore_signal(barrier, inc=1, device_id={"cols": z + 1}, device_id_type=MESH)

    sides = jnp.where(z > 0, 1, 0) + jnp.where(z < depth - 1, 1, 0)
    pl.semaphore_wait(barrier, n - 1 + sides)

    def row_copy(src, dst, send, recv, to):
        return pltpu.make_async_remote_copy(
            src_ref=src,
            dst_ref=dst,
            send_sem=send,
            recv_sem=recv,
            device_id={"rows": to},
            device_id_type=MESH,
        )

    far = [lax.rem(me + d, n) for d in range(1, n)]
    p1 = [
        row_copy(panel.at[to], ring_p.at[:, mine], p1_send.at[i], p1_recv.at[i], to)
        for i, to in enumerate(far)
    ]
    own_p1 = pltpu.make_async_copy(panel.at[me], ring_p.at[:, mine], local_sem.at[0])
    t1, own_t1 = [], []
    for c in range(chunks):
        span = pl.ds(c * part, part)
        t1.append(
            [
                row_copy(
                    trail.at[to, span],
                    rings[c].at[:, mine],
                    t1_send.at[c, i],
                    t1_recv.at[c, i],
                    to,
                )
                for i, to in enumerate(far)
            ]
        )
        own_t1.append(
            pltpu.make_async_copy(
                trail.at[me, span], rings[c].at[:, mine], local_sem.at[2 + c]
            )
        )
    p2 = [
        row_copy(moved_p.at[to], full.at[z, place], p2_send.at[i], p2_recv.at[i], to)
        for i, to in enumerate(far)
    ]
    t2 = [
        row_copy(moved_a.at[to], back.at[me], t2_send.at[i], t2_recv.at[i], to)
        for i, to in enumerate(far)
    ]
    own_t2 = pltpu.make_async_copy(moved_a.at[me], back.at[me], local_sem.at[2 + chunks])
    own_p2 = pltpu.make_async_copy(moved_p.at[me], full.at[z, place], local_sem.at[1])

    def line(side, d, q):
        step = 1 if side == 0 else -1
        origin = z - step * (d - 1)
        rows = pl.ds(q * width, width)
        return pltpu.make_async_remote_copy(
            src_ref=full.at[origin, rows],
            dst_ref=full.at[origin, rows],
            send_sem=z_send.at[side, d - 1, q],
            recv_sem=z_recv.at[side, d - 1, q],
            device_id={"cols": z + step},
            device_id_type=MESH,
        )

    def sends(side, d):
        if side == 0:
            return (z + 1 < depth) & (z - (d - 1) >= 0)
        return (z >= 1) & (z + (d - 1) < depth)

    def receives(side, d):
        return z - d >= 0 if side == 0 else z + d < depth

    def arrived(side, d, q):
        step = 1 if side == 0 else -1
        origin = z - step * d
        rows = pl.ds(q * width, width)
        return pltpu.make_async_remote_copy(
            src_ref=full.at[origin, rows],
            dst_ref=full.at[origin, rows],
            send_sem=z_send.at[side, d - 1, q],
            recv_sem=z_recv.at[side, d - 1, q],
            device_id={"cols": z - step},
            device_id_type=MESH,
        )

    def forward(d):
        for q in range(pieces):
            for side in (0, 1):

                @pl.when(receives(side, d))
                def _():
                    arrived(side, d, q).wait_recv()

                if d + 1 < depth:

                    @pl.when(sends(side, d + 1))
                    def _():
                        line(side, d + 1, q).start()

    own_p1.start()
    for copy in p1:
        copy.start()
    own_p1.wait()
    for copy in p1:
        copy.wait_recv()
    roll_rows(n, blocks, 0, kp, panel_shift, ring_p, moved_p)
    own_p2.start()
    for copy in p2:
        copy.start()
    for c in range(chunks):
        own_t1[c].start()
        for copy in t1[c]:
            copy.start()
    own_p2.wait()
    for copy in p2:
        copy.wait_recv()
    for q in range(pieces):
        for side in (0, 1):

            @pl.when(sends(side, 1))
            def _():
                line(side, 1, q).start()

    forward(1)
    own_t1[0].wait()
    for copy in t1[0]:
        copy.wait_recv()
    roll_rows(n, blocks, 0, part, trail_shift, rings[0], moved_a)
    own_t2.start()
    for copy in t2:
        copy.start()
    if depth > 2:
        forward(2)
    own_t1[1].wait()
    for copy in t1[1]:
        copy.wait_recv()
    roll_rows(n, blocks, part, part, trail_shift, rings[1], moved_b)
    for d in range(3, depth):
        forward(d)
    own_t2.wait()
    for copy in t2:
        copy.wait_recv()
    for copy in p1 + p2 + t1[0] + t1[1] + t2:
        copy.wait_send()
    for d in range(1, depth):
        for q in range(pieces):
            for side in (0, 1):

                @pl.when(sends(side, d))
                def _():
                    line(side, d, q).wait_send()


def exchange(panel, trail, panel_shift, trail_shift, n, depth):
    _, kp, blocks, _ = panel.shape
    kt = trail.shape[1]
    pieces = 4 if n % 4 == 0 else 1
    chunks = 2
    half = jax.ShapeDtypeStruct((n, kt // 2, blocks, BW), jnp.float32)
    f32 = jnp.float32
    smem = pl.BlockSpec(memory_space=pltpu.SMEM)
    vmem = pl.BlockSpec(memory_space=pltpu.VMEM)
    hbm = pl.BlockSpec(memory_space=pl.ANY)
    dma = pltpu.SemaphoreType.DMA
    return pl.pallas_call(
        functools.partial(exchange_kernel, n, depth, pieces, chunks),
        out_shape=(
            jax.ShapeDtypeStruct((depth, n * kp, blocks, BW), f32),
            half,
            half,
        ),
        in_specs=[smem, smem, hbm, hbm],
        out_specs=(vmem,) * 3,
        scratch_shapes=[
            pltpu.VMEM((kp, (n + 1) * blocks, BW), f32),
            pltpu.VMEM((n, kp, blocks, BW), f32),
            pltpu.VMEM(half.shape, f32),
            dma((n - 1,)),
            dma((n - 1,)),
            dma((chunks, n - 1)),
            dma((chunks, n - 1)),
            dma((n - 1,)),
            dma((n - 1,)),
            dma((n - 1,)),
            dma((n - 1,)),
            dma((2, max(depth - 1, 1), pieces)),
            dma((2, max(depth - 1, 1), pieces)),
            dma((3 + chunks,)),
        ]
        + [pltpu.VMEM((kt // chunks, (n + 1) * blocks, BW), f32)] * chunks,
        compiler_params=pltpu.CompilerParams(collective_id=3, has_side_effects=True),
        cost_estimate=pl.CostEstimate(
            flops=0, bytes_accessed=40 * trail.size * 4, transcendentals=0
        ),
    )(panel_shift, trail_shift, panel, trail)


def grouped(raw, shifts, n, my_row, unit):
    rows, pixels = raw.shape
    padded = -(-rows // (n * unit)) * n * unit
    if padded != rows:
        raw = jnp.pad(raw, ((0, padded - rows), (0, 0)))
        shifts = jnp.pad(shifts, (0, padded - rows))
    count = padded // n
    mine = lax.dynamic_slice_in_dim(shifts, my_row * count, count, 0)
    return raw.reshape(n, count, pixels // BW, BW), mine


def inner_rows(left, right, precision):
    return lax.dot_general(
        left,
        right,
        (((1,), (1,)), ((), ())),
        precision=precision,
        preferred_element_type=jnp.float32,
    )


def sum_kernel(n, part_ref, out_ref, landed, send_one, recv_one, send_two, recv_two):
    me = lax.axis_index("rows")
    barrier = pltpu.get_barrier_semaphore()
    for d in range(1, n):
        pl.semaphore_signal(
            barrier, inc=1, device_id={"rows": lax.rem(me + d, n)}, device_id_type=MESH
        )
    pl.semaphore_wait(barrier, n - 1)
    scatter = []
    for d in range(1, n):
        to = lax.rem(me + d, n)
        copy = pltpu.make_async_remote_copy(
            src_ref=part_ref.at[to],
            dst_ref=landed.at[d - 1],
            send_sem=send_one.at[d - 1],
            recv_sem=recv_one.at[d - 1],
            device_id={"rows": to},
            device_id_type=MESH,
        )
        copy.start()
        scatter.append(copy)
    total = part_ref[me]
    for d in range(1, n):
        scatter[d - 1].wait_recv()
        total = total + landed[d - 1]
    out_ref[me] = total
    spread = []
    for d in range(1, n):
        to = lax.rem(me + d, n)
        copy = pltpu.make_async_remote_copy(
            src_ref=out_ref.at[me],
            dst_ref=out_ref.at[me],
            send_sem=send_two.at[d - 1],
            recv_sem=recv_two.at[d - 1],
            device_id={"rows": to},
            device_id_type=MESH,
        )
        copy.start()
        spread.append(copy)
    for copy in scatter:
        copy.wait_send()
    for copy in spread:
        copy.wait_recv()
    for copy in spread:
        copy.wait_send()


def sum_rows(part, n, ident):
    rows, columns = part.shape
    cut = (n, rows // n, columns)
    out = pl.pallas_call(
        functools.partial(sum_kernel, n),
        out_shape=jax.ShapeDtypeStruct(cut, jnp.float32),
        in_specs=[pl.BlockSpec(memory_space=pltpu.VMEM)],
        out_specs=pl.BlockSpec(memory_space=pltpu.VMEM),
        scratch_shapes=[pltpu.VMEM((n - 1,) + cut[1:], jnp.float32)]
        + [pltpu.SemaphoreType.DMA((n - 1,))] * 4,
        compiler_params=pltpu.CompilerParams(collective_id=ident, has_side_effects=True),
        cost_estimate=pl.CostEstimate(
            flops=0, bytes_accessed=16 * part.size * 4, transcendentals=0
        ),
    )(part.reshape(cut))
    return out.reshape(rows, columns)


def factor_kernel(size, tile, scale, gram_ref, upper_ref, inv_ref, aug, pair):
    grow = lax.broadcasted_iota(jnp.int32, (size, size), 0)
    gcol = lax.broadcasted_iota(jnp.int32, (size, size), 1)
    aug[:, 0:size] = gram_ref[...]
    aug[:, size : 2 * size] = jnp.where(grow == gcol, 1.0, 0.0)
    row = lax.broadcasted_iota(jnp.int32, (tile, 2 * tile), 0)
    col = lax.broadcasted_iota(jnp.int32, (tile, 2 * tile), 1)
    for lo in range(0, size, tile):
        hi = lo + tile
        pair[...] = jnp.where(col == row + tile, 1.0, 0.0)
        pair[:, 0:tile] = aug[lo:hi, lo:hi]
        w = pair[...]
        pivots = jnp.zeros((tile, 1), jnp.float32)
        for j in range(tile):
            base = j // 8 * 8
            live = w[base:, :]
            lead = w[j : j + 1, :]
            pivot = lead[:, j : j + 1]
            pivots = jnp.where(row[:, 0:1] == j, pivot, pivots)
            if j + 1 == tile:
                break
            mult = jnp.where(row[base:, 0:1] > j, live[:, j : j + 1], 0.0)
            live = live - mult * (lead / pivot)
            w = live if base == 0 else jnp.concatenate([w[:base], live], axis=0)
        pair[...] = w * (1.0 / jnp.sqrt(pivots))
        inverse = pair[:, tile : 2 * tile]
        lead_rows = lax.dot_general(
            inverse,
            aug[lo:hi, :],
            (((1,), (0,)), ((), ())),
            precision=lax.Precision.HIGHEST,
            preferred_element_type=jnp.float32,
        )
        keep = gcol[lo:hi] >= grow[lo:hi]
        upper = jnp.where(keep, lead_rows[:, 0:size], 0.0)
        upper_ref[lo:hi, :] = upper * scale
        inv_ref[lo:hi, :] = lead_rows[:, size : 2 * size]
        if hi < size:
            aug[...] = aug[...] - lax.dot_general(
                upper,
                lead_rows,
                (((0,), (0,)), ((), ())),
                precision=lax.Precision.HIGHEST,
                preferred_element_type=jnp.float32,
            )


def factor(gram, scale):
    size = gram.shape[0]
    tile = min(64, size)
    square = jax.ShapeDtypeStruct((size, size), jnp.float32)
    return pl.pallas_call(
        functools.partial(factor_kernel, size, tile, scale),
        out_shape=(square, square),
        in_specs=[pl.BlockSpec(memory_space=pltpu.VMEM)],
        out_specs=(pl.BlockSpec(memory_space=pltpu.VMEM),) * 2,
        scratch_shapes=[
            pltpu.VMEM((size, 2 * size), jnp.float32),
            pltpu.VMEM((tile, 2 * tile), jnp.float32),
        ],
        cost_estimate=pl.CostEstimate(
            flops=2 * size**3, bytes_accessed=60 * size * size * 4, transcendentals=0
        ),
    )(gram)


def on_device(raw_panel, raw_trail, panel_shift, trail_shift):
    pcols = raw_panel.shape[0]
    pixels = raw_panel.shape[1]
    n = lax.axis_size("rows")
    my_row = lax.axis_index("rows")
    root = math.sqrt(pixels * n)
    depth = lax.axis_size("cols")
    trows = raw_trail.shape[0]
    panel, panel_mine = grouped(raw_panel, panel_shift, n, my_row, 1)
    trail, trail_mine = grouped(raw_trail, trail_shift, n, my_row, 2)
    full, front, moved = exchange(panel, trail, panel_mine, trail_mine, n, depth)
    full_panel = full.reshape(depth, -1, pixels)[:, :pcols].reshape(depth * pcols, pixels)
    full_panel = lax.optimization_barrier(full_panel)
    gram = sum_rows(inner_rows(full_panel, full_panel, lax.Precision.HIGHEST), n, 1)
    gram, moved = lax.optimization_barrier((gram, moved))
    rest = lax.all_to_all(moved, "rows", split_axis=0, concat_axis=0, tiled=True)
    reg_trail = jnp.concatenate([front, rest], axis=1).reshape(-1, pixels)[:trows]
    reg_trail = lax.optimization_barrier(reg_trail)
    r_factor, inverse = factor(gram, 1.0 / root)
    cross = sum_rows(inner_rows(full_panel, reg_trail, lax.Precision.HIGH), n, 2)
    highest = lax.Precision.HIGHEST
    coupling = jnp.dot(inverse, cross, precision=highest, preferred_element_type=jnp.float32)
    weights = lax.dot_general(
        inverse,
        coupling,
        (((0,), (0,)), ((), ())),
        precision=highest,
        preferred_element_type=jnp.float32,
    )
    removed = lax.dot_general(
        weights,
        full_panel,
        (((0,), (0,)), ((), ())),
        precision=lax.Precision.HIGH,
        preferred_element_type=jnp.float32,
    )
    trail_out = reg_trail - removed
    own = lax.dynamic_slice_in_dim(inverse, lax.axis_index("cols") * pcols, pcols, 0)
    q_panel = jnp.dot(
        own * root, full_panel, precision=lax.Precision.HIGH, preferred_element_type=jnp.float32
    )
    return (r_factor, coupling / root, q_panel, trail_out)


def solution(mesh):
    placed = (P("cols", "rows"), P("cols", "rows"), P("cols"), P("cols"))
    return jax.shard_map(
        on_device,
        mesh=mesh,
        in_specs=placed,
        out_specs=(P(), P(None, "cols"), P("cols", "rows"), P("cols", "rows")),
        check_vma=False,
    )
```
